256 devices in a mesh: panel: 8 (over x, core), front: 32 (over z, y).
Axes of the slice: x: 4, y: 4, z: 8, core: 2. Of those that a mesh axis runs over, the one named last changes fastest.
Arguments:
- rhs: float32 [8, 64, 64, 2, 128], P('panel', None, 'front'), may hold values from -6 to 6
- fronts: bfloat16 [8, 2, 8192, 8192], P('panel', None, 'front'), may hold values from -0.046875 to 0.046875
- wave_sq: float32 [8, 64, 128], P('panel', 'front'), may hold values from 0.5 to 2
- pml_width: int32 [8], P('panel'), may hold values from 1 to 16
Outputs:
- sweep_field: float32 [8, 64, 64, 2, 128], P('panel', None, 'front')
- residual: float32 [8, 64, 64, 2, 128], P('panel', None, 'front')
The draws below stay inside these ranges and needn't reach their ends.
All inputs are finite; a program needn't handle non-finite values.
Results may differ from the reference program's by a relative error of at most 0.013.
Values may be sent and summed in bfloat16 or wider, within the bound.
A program may use at most 64 MiB of HBM per device.

```python
import jax
import jax.numpy as jnp

NRHS = 64
PX = 64
PY = 128
CF = 8192
FRONT = 16384
NQ = 8


def place_ends(array, key, least, top_value):
    index_at = [jax.random.randint(jax.random.fold_in(key, axis), (), 0, length) for axis, length in enumerate(array.shape)]
    widest = array.shape.index(max(array.shape))
    beside = index_at[:widest] + [(index_at[widest] + 1) % array.shape[widest]] + index_at[widest + 1:]
    return array.at[tuple(index_at)].set(least).at[tuple(beside)].set(top_value)


def block_levels(key, shape, pieces, low, top_value):
    def one(position, parts):
        draws = jax.random.uniform(jax.random.fold_in(jax.random.fold_in(key, 6), position), (parts,), jnp.float32, low / len(pieces), top_value / len(pieces))
        return jnp.repeat(jnp.exp(draws), shape[position] // parts).reshape((-1,) + (1,) * (len(shape) - position - 1))

    level = one(*pieces[0])
    for cut in pieces[1:]:
        level = level * one(*cut)
    return level


def bell_draw(own_key, dims, scale, limit, pieces=(), kind=jnp.bfloat16):
    array = jax.random.normal(own_key, dims, jnp.float32) * scale
    if len(pieces) > 0:
        array = block_levels(own_key, dims, pieces, -0.22, 0.18) * array
    return jnp.clip(array, min=-limit, max=limit).astype(kind)


def setup_inputs(seed: int = 0) -> dict:
    keys = jax.random.split(jax.random.key(seed), 5)
    return {
        "rhs": bell_draw(keys[0], (NQ, NRHS, PX, 2, PY), 1.0, 6.0, ((0, 8), (2, 32)), jnp.float32),
        "fronts": bell_draw(keys[1], (NQ, 2, CF, CF), FRONT ** -0.5, 0.046875, ((0, 8), (2, 32))),
        "wave_sq": jnp.clip(0.5 + 1.5 * jax.random.uniform(keys[2], (NQ, PX, PY), jnp.float32) ** block_levels(keys[2], (NQ, PX, PY), ((0, 8), (1, 32)), -0.2, 0.2), 0.5, 2.0),
        "pml_width": place_ends(jax.random.randint(keys[3], (NQ,), 1, PX // 4 + 1), jax.random.fold_in(keys[3], 1), 1, (PX // 4 + 1) - 1).astype(jnp.int32),
    }


def reference(rhs, fronts, wave_sq, pml_width):
    carried = jnp.zeros((NRHS, PX, 2, PY), jnp.float32)
    solved_list = []
    for panel_num in range(NQ):
        combined = (rhs[panel_num] + carried).astype(jnp.bfloat16)
        x_re = combined[:, :, 0].reshape(NRHS, CF)
        x_im = combined[:, :, 1].reshape(NRHS, CF)
        c_re = fronts[panel_num, 0].T
        c_im = fronts[panel_num, 1].T
        out_re = jnp.dot(x_re, c_re, preferred_element_type=jnp.float32) - jnp.dot(x_im, c_im, preferred_element_type=jnp.float32)
        out_im = jnp.dot(x_re, c_im, preferred_element_type=jnp.float32) + jnp.dot(x_im, c_re, preferred_element_type=jnp.float32)
        solved = jnp.stack([out_re.reshape(NRHS, PX, PY), out_im.reshape(NRHS, PX, PY)], axis=2)
        solved_list.append(solved)
        carried = solved
    sweep_field = jnp.stack(solved_list)
    row_pos = jnp.arange(PX, dtype=jnp.float32)[None, :]
    thick = pml_width.astype(jnp.float32)[:, None]
    absorb = 2.0 * (jnp.maximum(0.0, thick - row_pos) + jnp.maximum(0.0, row_pos - (PX - 1 - thick))) / thick
    padded = jnp.pad(sweep_field, ((1, 1), (0, 0), (1, 1), (0, 0), (1, 1)))
    beside = padded[2:, :, 1:-1, :, 1:-1] + padded[:-2, :, 1:-1, :, 1:-1]
    beside = beside + padded[1:-1, :, 2:, :, 1:-1] + padded[1:-1, :, :-2, :, 1:-1]
    beside = beside + padded[1:-1, :, 1:-1, :, 2:] + padded[1:-1, :, 1:-1, :, :-2]
    diagonal_term = (6.0 - wave_sq)[:, None, :, :]
    absorb_b = absorb[:, None, :, None]
    real_part = sweep_field[:, :, :, 0]
    imag_part = sweep_field[:, :, :, 1]
    apply_re = diagonal_term * real_part - absorb_b * imag_part - beside[:, :, :, 0]
    apply_im = diagonal_term * imag_part + absorb_b * real_part - beside[:, :, :, 1]
    residual = rhs - jnp.stack([apply_re, apply_im], axis=3)
    return sweep_field, residual
```

```python
import functools

import jax
import jax.numpy as jnp
from jax import lax
from jax.experimental import pallas as pl
from jax.experimental.pallas import tpu as pltpu
from jax.sharding import PartitionSpec as P

MESH = pl.DeviceIdType.MESH
NY = 4
NZ = 8
BLOCKS = 8


def kernel(
    panels,
    rhs_ref,
    fronts_ref,
    wave_ref,
    pml_ref,
    field_ref,
    resid_ref,
    cs,
    xs,
    piece,
    swept,
    rhs_next,
    before,
    behind,
    above,
    below,
    cs_sem,
    a_send,
    a_recv,
    b_send,
    b_recv,
    n_send,
    n_recv,
    h_send,
    h_recv,
):
    blocks = xs.shape[0]
    rows2 = xs.shape[3]
    per = rows2 // 2
    piece_cols = xs.shape[4]
    columns = rhs_ref.shape[1]
    rhs_count = rhs_ref.shape[0] // 4
    fronts_n = NY * NZ

    q = lax.axis_index("panel")
    f = lax.axis_index("front")
    z = f // NY
    y = f % NY

    def peer(panel, zz, yy):
        return (panel, zz * NY + yy)

    @pl.loop(0, fronts_n)
    def _(k):
        yy = (y + k // NZ) % NY
        zz = k % NZ
        pltpu.make_async_copy(
            fronts_ref.at[:, :, pl.ds(pl.multiple_of((zz * NY + yy) * piece_cols, piece_cols), piece_cols)],
            cs.at[yy, :, :, pl.ds(pl.multiple_of(zz * piece_cols, piece_cols), piece_cols)],
            cs_sem,
        ).start()

    barrier = pltpu.get_barrier_semaphore()

    def greet(target):
        pl.semaphore_signal(barrier, inc=1, device_id=target, device_id_type=MESH)

    for j in range(1, NY):
        greet(peer(q, z, (y + j) % NY))

    @pl.when(q > 0)
    def _():
        for zz in range(NZ):
            greet(peer(q - 1, zz, y))

    @pl.when(q < panels - 1)
    def _():
        for zz in range(NZ):
            greet(peer(q + 1, zz, y))

    @pl.when(q == 0)
    def _():
        for j in range(1, NZ):
            greet(peer(q, (z + j) % NZ, y))

    @pl.when(f > 0)
    def _():
        greet((q, f - 1))

    @pl.when(f < fronts_n - 1)
    def _():
        greet((q, f + 1))

    def rhs_rows(ref, b, row, part):
        return ref[pl.ds(b * (per * 4) + row * 2 + part, per, stride=4), :]

    def as_piece(b, ref, field):
        parts = []
        for part in range(2):
            halves = [rhs_rows(ref, b, row, part) for row in range(2)]
            value = jnp.concatenate(halves, axis=1)
            if field is not None:
                value = value + field[part]
            parts.append(value)
        return jnp.concatenate(parts, axis=0).astype(jnp.bfloat16)

    @pl.when(q == 0)
    def _():
        @pl.loop(0, blocks)
        def _(b):
            piece[b] = as_piece(b, rhs_ref, None)

    @pl.when(f == 0)
    def _():
        above[...] = jnp.zeros_like(above)

    @pl.when(f == fronts_n - 1)
    def _():
        below[...] = jnp.zeros_like(below)

    @pl.when(q == 0)
    def _():
        before[...] = jnp.zeros_like(before)

    @pl.when(q == panels - 1)
    def _():
        behind[...] = jnp.zeros_like(behind)

    expected = (
        NY
        - 1
        + jnp.where(q > 0, NZ, NZ - 1)
        + jnp.where(q < panels - 1, NZ, 0)
        + jnp.where(f > 0, 1, 0)
        + jnp.where(f < fronts_n - 1, 1, 0)
    )
    pl.semaphore_wait(barrier, expected)

    def send_piece(b, panel, zz):
        return pltpu.make_async_remote_copy(
            src_ref=piece.at[b],
            dst_ref=xs.at[b, y, z],
            send_sem=a_send.at[b],
            recv_sem=a_recv.at[b],
            device_id=peer(panel, zz, y),
            device_id_type=MESH,
        )

    far_first = (4, 3, 5, 2, 6, 1, 7, 0)

    @pl.when(q == 0)
    def _():
        @pl.loop(0, blocks)
        def _(b):
            for j in far_first[:-1]:
                send_piece(b, q, (z + j) % NZ).start()
            pltpu.make_async_copy(piece.at[b], xs.at[b, y, z], a_recv.at[b]).start()

    def send_rhs():
        return pltpu.make_async_remote_copy(
            src_ref=rhs_ref,
            dst_ref=rhs_next,
            send_sem=n_send,
            recv_sem=n_recv,
            device_id=(q - 1, f),
            device_id_type=MESH,
        )

    @pl.when(q > 0)
    def _():
        send_rhs().start()

    def send_bundle(b, j):
        return pltpu.make_async_remote_copy(
            src_ref=xs.at[b, y],
            dst_ref=xs.at[b, y],
            send_sem=b_send.at[b, j],
            recv_sem=b_recv.at[b, y],
            device_id=peer(q, z, (y + j) % NY),
            device_id_type=MESH,
        )

    def bundle_wait(b, sem):
        pltpu.make_async_copy(xs.at[b, y], xs.at[b, y], sem).wait()

    def gather_and_forward(b):
        bundle_wait(b, a_recv.at[b])
        for j in (2, 1, 3):
            send_bundle(b, j).start()

    def times_front(b, yy):
        vectors = jnp.concatenate([xs[b, yy, zz] for zz in range(NZ)], axis=1)
        block = cs[yy].reshape(2 * piece_cols, NZ * piece_cols)
        return lax.dot_general(
            vectors, block, (((1,), (1,)), ((), ())), preferred_element_type=jnp.float32
        )

    gather_and_forward(0)
    pltpu.make_async_copy(cs, cs, cs_sem).wait()

    @pl.when(q < panels - 1)
    def _():
        pltpu.make_async_copy(rhs_next, rhs_next, n_recv).wait()

    @pl.loop(0, blocks)
    def _(b):
        total = times_front(b, y)

        @pl.when(b + 1 < blocks)
        def _():
            gather_and_forward(b + 1)

        for j in (1, 3, 2):
            yy = (y + j) % NY
            pltpu.make_async_copy(xs.at[b, yy], xs.at[b, yy], b_recv.at[b, yy]).wait()
            total = total + times_front(b, yy)
        re = total[:per, :piece_cols] - total[per:, piece_cols:]
        im = total[:per, piece_cols:] + total[per:, :piece_cols]

        @pl.when(q < panels - 1)
        def _():
            piece_at = jnp.where(q == 0, blocks + b, b)
            piece[piece_at] = as_piece(b, rhs_next, (re, im))
            for j in far_first:
                pltpu.make_async_remote_copy(
                    src_ref=piece.at[piece_at],
                    dst_ref=xs.at[b, y, z],
                    send_sem=a_send.at[piece_at],
                    recv_sem=a_recv.at[b],
                    device_id=peer(q + 1, (z + j) % NZ, y),
                    device_id_type=MESH,
                ).start()

        for part, value in ((0, re), (1, im)):
            for row in range(2):
                field_ref[pl.ds(b * (per * 4) + row * 2 + part, per, stride=4), :] = value[
                    :, row * columns : (row + 1) * columns
                ]
        swept[b] = jnp.concatenate([re, im], axis=0).astype(jnp.bfloat16)

    def halo(src, dst, at, target):
        return pltpu.make_async_remote_copy(
            src_ref=src,
            dst_ref=dst,
            send_sem=h_send.at[at],
            recv_sem=h_recv.at[at],
            device_id=target,
            device_id_type=MESH,
        )

    to_before = halo(swept, behind, 0, (q - 1, f))
    to_behind = halo(swept, before, 1, (q + 1, f))
    to_above = halo(swept.at[:, :, pl.ds(0, columns)], below, 2, (q, f - 1))
    to_below = halo(swept.at[:, :, pl.ds(columns, columns)], above, 3, (q, f + 1))
    has_before, has_behind = q > 0, q < panels - 1
    has_above, has_below = f > 0, f < fronts_n - 1
    sides = (
        (to_before, has_before, has_behind),
        (to_behind, has_behind, has_before),
        (to_above, has_above, has_below),
        (to_below, has_below, has_above),
    )
    for copy, sends, _ in sides:
        pl.when(sends)(copy.start)
    for copy, _, receives in sides:
        pl.when(receives)(copy.wait_recv)

    lane = lax.broadcasted_iota(jnp.int32, (rhs_count, columns), 1)

    def from_halo(ref, part, lo):
        return ref[:, :, lo : lo + columns].astype(jnp.float32)[
            :, part * per : (part + 1) * per
        ].reshape(rhs_count, columns)

    thick = jnp.full((1, columns), pml_ref[0], jnp.int32).astype(jnp.float32)
    last_row = fronts_n * 2 - 1
    field = [
        [field_ref[pl.ds(row * 2 + part, rhs_count, stride=4), :] for part in range(2)]
        for row in range(2)
    ]
    for row in range(2):
        row_pos = jnp.full((1, columns), f * 2 + row, jnp.int32).astype(jnp.float32)
        absorb = (
            2.0
            * (jnp.maximum(0.0, thick - row_pos) + jnp.maximum(0.0, row_pos - (last_row - thick)))
            / thick
        )
        diagonal = 6.0 - wave_ref[row : row + 1, :]
        for part in range(2):
            u = field[row][part]
            beside = from_halo(behind, part, row * columns) + from_halo(before, part, row * columns)
            if row == 0:
                beside = beside + field[1][part] + from_halo(above, part, 0)
            else:
                beside = beside + from_halo(below, part, 0) + field[0][part]
            right = jnp.where(lane == columns - 1, 0.0, pltpu.roll(u, columns - 1, 1))
            left = jnp.where(lane == 0, 0.0, pltpu.roll(u, 1, 1))
            beside = beside + right + left
            other = absorb * field[row][1 - part]
            applied = diagonal * u + (other if part == 1 else -other) - beside
            at = pl.ds(row * 2 + part, rhs_count, stride=4)
            resid_ref[at, :] = rhs_ref[at, :] - applied

    for copy, sends, _ in sides:
        pl.when(sends)(copy.wait_send)

    @pl.when(q > 0)
    def _():
        send_rhs().wait_send()

    @pl.loop(0, blocks)
    def _(b):
        for j in range(1, NY):
            send_bundle(b, j).wait_send()

        @pl.when(q == 0)
        def _():
            part = xs.at[b, y, pl.ds(0, NZ - 1)]
            pltpu.make_async_copy(part, part, a_send.at[b]).wait()

        @pl.when(q < panels - 1)
        def _():
            bundle_wait(b, a_send.at[jnp.where(q == 0, blocks + b, b)])


def local(rhs, fronts, wave_sq, pml_width):
    _, rhs_count, row_count, components, columns = rhs.shape
    panels = lax.axis_size("panel")
    rows = rhs_count * row_count * components
    piece_cols = row_count * columns
    rows2 = components * rhs_count // BLOCKS
    bf16, f32 = jnp.bfloat16, jnp.float32
    dma = pltpu.SemaphoreType.DMA
    vmem = pl.BlockSpec(memory_space=pltpu.VMEM)
    field, resid = pl.pallas_call(
        functools.partial(kernel, panels),
        out_shape=(jax.ShapeDtypeStruct((rows, columns), f32),) * 2,
        in_specs=[
            vmem,
            pl.BlockSpec(memory_space=pltpu.HBM),
            vmem,
            pl.BlockSpec(memory_space=pltpu.SMEM),
        ],
        out_specs=(vmem, vmem),
        scratch_shapes=[
            pltpu.VMEM((NY, 2, piece_cols, NZ * piece_cols), bf16),
            pltpu.VMEM((BLOCKS, NY, NZ, rows2, piece_cols), bf16),
            pltpu.VMEM((2 * BLOCKS, rows2, piece_cols), bf16),
            pltpu.VMEM((BLOCKS, rows2, piece_cols), bf16),
            pltpu.VMEM((rows, columns), f32),
            pltpu.VMEM((BLOCKS, rows2, piece_cols), bf16),
            pltpu.VMEM((BLOCKS, rows2, piece_cols), bf16),
            pltpu.VMEM((BLOCKS, rows2, columns), bf16),
            pltpu.VMEM((BLOCKS, rows2, columns), bf16),
            dma,
            dma((2 * BLOCKS,)),
            dma((BLOCKS,)),
            dma((BLOCKS, NY)),
            dma((BLOCKS, NY)),
            dma,
            dma,
            dma((4,)),
            dma((4,)),
        ],
        compiler_params=pltpu.CompilerParams(
            collective_id=0, has_side_effects=True, vmem_limit_bytes=32 * 1024 * 1024
        ),
    )(
        rhs.reshape(rows, columns),
        fronts.reshape(fronts.shape[1:]),
        wave_sq.reshape(row_count, columns),
        pml_width,
    )
    return field.reshape(rhs.shape), resid.reshape(rhs.shape)


def solution(mesh):
    return jax.shard_map(
        local,
        mesh=mesh,
        in_specs=(
            P("panel", None, "front", None, None),
            P("panel", None, "front", None),
            P("panel", "front", None),
            P("panel"),
        ),
        out_specs=(P("panel", None, "front", None, None), P("panel", None, "front", None, None)),
        check_vma=False,
    )
```

```python
import functools

import jax
import jax.numpy as jnp
from jax import lax
from jax.experimental import pallas as pl
from jax.experimental.pallas import tpu as pltpu
from jax.sharding import PartitionSpec as P

MESH = pl.DeviceIdType.MESH
NY = 4
NZ = 8
BLOCKS = 8
NEAR = 5


def slot_of(dz):
    return (dz + 2) % NZ


def kernel(
    panels,
    rhs_hbm,
    fronts_hbm,
    wave_hbm,
    pml_ref,
    field_ref,
    resid_ref,
    rhs_ref,
    wave_ref,
    cs,
    xs,
    piece,
    swept,
    rhs_next,
    before,
    behind,
    above,
    below,
    rhs_sem,
    wave_sem,
    cs_sem,
    a_send,
    a_recv,
    b_send,
    b_recv,
    n_send,
    n_recv,
    h_send,
    h_recv,
):
    blocks = xs.shape[0]
    rows2 = xs.shape[3]
    per = rows2 // 2
    piece_cols = xs.shape[4]
    columns = rhs_ref.shape[1]
    fronts_n = NY * NZ
    groups = (pl.ds(0, NEAR), pl.ds(NEAR, NZ - NEAR))

    q = lax.axis_index("panel")
    f = lax.axis_index("front")
    z = f // NY
    y = f % NY

    def peer(panel, zz, yy):
        return (panel, zz * NY + yy)

    barrier = pltpu.get_barrier_semaphore()

    def greet(target):
        pl.semaphore_signal(barrier, inc=1, device_id=target, device_id_type=MESH)

    far_first = (4, 3, 5, 2, 6, 1, 7, 0)

    @pl.when(q == 0)
    def _():
        for j in far_first[:-1]:
            greet(peer(q, (z + j) % NZ, y))

    @pl.when(q < panels - 1)
    def _():
        for j in far_first:
            greet(peer(q + 1, (z + j) % NZ, y))

    @pl.when(q > 0)
    def _():
        for j in far_first:
            greet(peer(q - 1, (z + j) % NZ, y))

    for k in range(1, NY):
        greet(peer(q, z, (y + k) % NY))

    @pl.when(f > 0)
    def _():
        greet((q, f - 1))

    @pl.when(f < fronts_n - 1)
    def _():
        greet((q, f + 1))

    rhs_in = pltpu.make_async_copy(rhs_hbm, rhs_ref, rhs_sem)
    wave_in = pltpu.make_async_copy(wave_hbm, wave_ref, wave_sem)
    rhs_in.start()
    wave_in.start()

    @pl.loop(0, fronts_n)
    def _(k):
        dy = k // NZ
        slot = k % NZ
        at = ((z + slot + NZ - 2) % NZ) * NY + (y + dy) % NY
        pltpu.make_async_copy(
            fronts_hbm.at[:, :, pl.ds(pl.multiple_of(at * piece_cols, piece_cols), piece_cols)],
            cs.at[dy, :, :, pl.ds(pl.multiple_of(slot * piece_cols, piece_cols), piece_cols)],
            cs_sem,
        ).start()

    def rhs_rows(ref, b, row, part):
        return ref[pl.ds(b * (per * 4) + row * 2 + part, per, stride=4), :]

    def as_piece(b, ref, field):
        parts = []
        for part in range(2):
            halves = [rhs_rows(ref, b, row, part) for row in range(2)]
            value = jnp.concatenate(halves, axis=1)
            if field is not None:
                value = value + field[part]
            parts.append(value)
        return jnp.concatenate(parts, axis=0).astype(jnp.bfloat16)

    rhs_in.wait()

    @pl.when(q == 0)
    def _():
        @pl.loop(0, blocks)
        def _(b):
            piece[b] = as_piece(b, rhs_ref, None)

    @pl.when(f == 0)
    def _():
        above[...] = jnp.zeros_like(above)

    @pl.when(f == fronts_n - 1)
    def _():
        below[...] = jnp.zeros_like(below)

    @pl.when(q == 0)
    def _():
        before[...] = jnp.zeros_like(before)

    @pl.when(q == panels - 1)
    def _():
        behind[...] = jnp.zeros_like(behind)

    expected = (
        NY
        - 1
        + jnp.where(q > 0, NZ, NZ - 1)
        + jnp.where(q < panels - 1, NZ, 0)
        + jnp.where(f > 0, 1, 0)
        + jnp.where(f < fronts_n - 1, 1, 0)
    )
    pl.semaphore_wait(barrier, expected)

    def send_piece(b, source, panel, j):
        slot = slot_of(-j % NZ)
        return pltpu.make_async_remote_copy(
            src_ref=piece.at[source],
            dst_ref=xs.at[b, 0, slot],
            send_sem=a_send.at[source],
            recv_sem=a_recv.at[b, 0 if slot < NEAR else 1],
            device_id=peer(panel, (z + j) % NZ, y),
            device_id_type=MESH,
        )

    @pl.when(q == 0)
    def _():
        @pl.loop(0, blocks)
        def _(b):
            for j in far_first[:-1]:
                send_piece(b, b, q, j).start()
            own = xs.at[b, 0, slot_of(0)]
            pltpu.make_async_copy(piece.at[b], own, a_recv.at[b, 0]).start()

    def send_rhs():
        return pltpu.make_async_remote_copy(
            src_ref=rhs_ref,
            dst_ref=rhs_next,
            send_sem=n_send,
            recv_sem=n_recv,
            device_id=(q - 1, f),
            device_id_type=MESH,
        )

    @pl.when(q > 0)
    def _():
        send_rhs().start()

    def send_group(b, k, g):
        dy = -k % NY
        return pltpu.make_async_remote_copy(
            src_ref=xs.at[b, 0, groups[g]],
            dst_ref=xs.at[b, dy, groups[g]],
            send_sem=b_send.at[b, k, g],
            recv_sem=b_recv.at[b, dy, g],
            device_id=peer(q, z, (y + k) % NY),
            device_id_type=MESH,
        )

    def bytes_wait(ref, sem):
        pltpu.make_async_copy(ref, ref, sem).wait()

    def forward(b, g):
        bytes_wait(xs.at[b, 0, groups[g]], a_recv.at[b, g])
        for k in (2, 1, 3):
            send_group(b, k, g).start()

    def times_front(b, dy, g):
        lo, hi = (0, NEAR) if g == 0 else (NEAR, NZ)
        vectors = jnp.concatenate([xs[b, dy, slot] for slot in range(lo, hi)], axis=1)
        block = cs[dy, :, :, lo * piece_cols : hi * piece_cols]
        return lax.dot_general(
            vectors,
            block.reshape(2 * piece_cols, (hi - lo) * piece_cols),
            (((1,), (1,)), ((), ())),
            preferred_element_type=jnp.float32,
        )

    def arrived(b, dy, g):
        bytes_wait(xs.at[b, dy, groups[g]], b_recv.at[b, dy, g])
        return times_front(b, dy, g)

    has_before, has_behind = q > 0, q < panels - 1
    has_above, has_below = f > 0, f < fronts_n - 1
    parts_of = (pl.ds(0, blocks - 1), pl.ds(blocks - 1, 1))

    def halos(p):
        def halo(src, dst, at, target):
            return pltpu.make_async_remote_copy(
                src_ref=src,
                dst_ref=dst,
                send_sem=h_send.at[p, at],
                recv_sem=h_recv.at[p, at],
                device_id=target,
                device_id_type=MESH,
            )

        some = parts_of[p]
        return (
            (halo(swept.at[some], behind.at[some], 0, (q - 1, f)), has_before, has_behind),
            (halo(swept.at[some], before.at[some], 1, (q + 1, f)), has_behind, has_before),
            (
                halo(swept.at[some, :, pl.ds(0, columns)], below.at[some], 2, (q, f - 1)),
                has_above,
                has_below,
            ),
            (
                halo(swept.at[some, :, pl.ds(columns, columns)], above.at[some], 3, (q, f + 1)),
                has_below,
                has_above,
            ),
        )

    def send_halos(p):
        for copy, sends, _ in halos(p):
            pl.when(sends)(copy.start)

    forward(0, 0)
    forward(0, 1)
    bytes_wait(cs, cs_sem)

    @pl.when(q < panels - 1)
    def _():
        bytes_wait(rhs_next, n_recv)

    @pl.loop(0, blocks)
    def _(b):
        total = times_front(b, 0, 0) + times_front(b, 0, 1)

        @pl.when(b + 1 < blocks)
        def _():
            forward(b + 1, 0)

        for dy in (1, 3, 2):
            total = total + arrived(b, dy, 0)

        @pl.when(b + 1 < blocks)
        def _():
            forward(b + 1, 1)

        for dy in (1, 3, 2):
            total = total + arrived(b, dy, 1)
        re = total[:per, :piece_cols] - total[per:, piece_cols:]
        im = total[:per, piece_cols:] + total[per:, :piece_cols]

        @pl.when(q < panels - 1)
        def _():
            source = jnp.where(q == 0, blocks + b, b)
            piece[source] = as_piece(b, rhs_next, (re, im))
            for j in far_first:
                send_piece(b, source, q + 1, j).start()

        swept[b] = jnp.concatenate([re, im], axis=0).astype(jnp.bfloat16)
        for part, value in ((0, re), (1, im)):
            for row in range(2):
                field_ref[pl.ds(b * (per * 4) + row * 2 + part, per, stride=4), :] = value[
                    :, row * columns : (row + 1) * columns
                ]

        @pl.when(b == blocks - 2)
        def _():
            send_halos(0)

    send_halos(1)
    wave_in.wait()
    thick = jnp.full((1, columns), pml_ref[0], jnp.int32).astype(jnp.float32)
    last_row = fronts_n * 2 - 1

    def residual_of(p):
        first, count = (0, blocks - 1) if p == 0 else (blocks - 1, 1)
        rhs_count = count * per
        some = parts_of[p]
        for copy, _, receives in halos(p):
            pl.when(receives)(copy.wait_recv)
        lane = lax.broadcasted_iota(jnp.int32, (rhs_count, columns), 1)

        def at(row, part):
            return pl.ds(first * per * 4 + row * 2 + part, rhs_count, stride=4)

        def from_halo(ref, part, lo):
            values = ref[some, :, lo : lo + columns].astype(jnp.float32)
            return values[:, part * per : (part + 1) * per].reshape(rhs_count, columns)

        field = [[field_ref[at(row, part), :] for part in range(2)] for row in range(2)]
        for row in range(2):
            row_pos = jnp.full((1, columns), f * 2 + row, jnp.int32).astype(jnp.float32)
            absorb = (
                2.0
                * (
                    jnp.maximum(0.0, thick - row_pos)
                    + jnp.maximum(0.0, row_pos - (last_row - thick))
                )
                / thick
            )
            diagonal = 6.0 - wave_ref[row : row + 1, :]
            for part in range(2):
                u = field[row][part]
                beside = from_halo(behind, part, row * columns)
                beside = beside + from_halo(before, part, row * columns)
                if row == 0:
                    beside = beside + field[1][part] + from_halo(above, part, 0)
                else:
                    beside = beside + from_halo(below, part, 0) + field[0][part]
                right = jnp.where(lane == columns - 1, 0.0, pltpu.roll(u, columns - 1, 1))
                left = jnp.where(lane == 0, 0.0, pltpu.roll(u, 1, 1))
                beside = beside + right + left
                other = absorb * field[row][1 - part]
                applied = diagonal * u + (other if part == 1 else -other) - beside
                resid_ref[at(row, part), :] = rhs_ref[at(row, part), :] - applied

    residual_of(0)
    residual_of(1)

    for p in range(2):
        for copy, sends, _ in halos(p):
            pl.when(sends)(copy.wait_send)

    @pl.when(q > 0)
    def _():
        send_rhs().wait_send()

    @pl.loop(0, blocks)
    def _(b):
        for g in range(2):
            for k in range(1, NY):
                send_group(b, k, g).wait_send()

        @pl.when(q == 0)
        def _():
            bytes_wait(xs.at[b, 0, pl.ds(0, NZ - 1)], a_send.at[b])

        @pl.when(q < panels - 1)
        def _():
            bytes_wait(xs.at[b, 0], a_send.at[jnp.where(q == 0, blocks + b, b)])


def local(rhs, fronts, wave_sq, pml_width):
    _, rhs_count, row_count, components, columns = rhs.shape
    panels = lax.axis_size("panel")
    rows = rhs_count * row_count * components
    piece_cols = row_count * columns
    rows2 = components * rhs_count // BLOCKS
    bf16, f32 = jnp.bfloat16, jnp.float32
    dma = pltpu.SemaphoreType.DMA
    vmem = pl.BlockSpec(memory_space=pltpu.VMEM)
    anywhere = pl.BlockSpec(memory_space=pl.ANY)
    field, resid = pl.pallas_call(
        functools.partial(kernel, panels),
        out_shape=(jax.ShapeDtypeStruct((rows, columns), f32),) * 2,
        in_specs=[anywhere, anywhere, anywhere, pl.BlockSpec(memory_space=pltpu.SMEM)],
        out_specs=(vmem, vmem),
        scratch_shapes=[
            pltpu.VMEM((rows, columns), f32),
            pltpu.VMEM((row_count, columns), f32),
            pltpu.VMEM((NY, 2, piece_cols, NZ * piece_cols), bf16),
            pltpu.VMEM((BLOCKS, NY, NZ, rows2, piece_cols), bf16),
            pltpu.VMEM((2 * BLOCKS, rows2, piece_cols), bf16),
            pltpu.VMEM((BLOCKS, rows2, piece_cols), bf16),
            pltpu.VMEM((rows, columns), f32),
            pltpu.VMEM((BLOCKS, rows2, piece_cols), bf16),
            pltpu.VMEM((BLOCKS, rows2, piece_cols), bf16),
            pltpu.VMEM((BLOCKS, rows2, columns), bf16),
            pltpu.VMEM((BLOCKS, rows2, columns), bf16),
            dma,
            dma,
            dma,
            dma((2 * BLOCKS,)),
            dma((BLOCKS, 2)),
            dma((BLOCKS, NY, 2)),
            dma((BLOCKS, NY, 2)),
            dma,
            dma,
            dma((2, 4)),
            dma((2, 4)),
        ],
        compiler_params=pltpu.CompilerParams(
            collective_id=0, has_side_effects=True, vmem_limit_bytes=63 * 1024 * 1024
        ),
    )(
        rhs.reshape(rows, columns),
        fronts.reshape(fronts.shape[1:]),
        wave_sq.reshape(row_count, columns),
        pml_width,
    )
    return field.reshape(rhs.shape), resid.reshape(rhs.shape)


def solution(mesh):
    return jax.shard_map(
        local,
        mesh=mesh,
        in_specs=(
            P("panel", None, "front", None, None),
            P("panel", None, "front", None),
            P("panel", "front", None),
            P("panel"),
        ),
        out_specs=(P("panel", None, "front", None, None), P("panel", None, "front", None, None)),
        check_vma=False,
    )
```

```python
import functools

import jax
import jax.numpy as jnp
from jax import lax
from jax.experimental import pallas as pl
from jax.experimental.pallas import tpu as pltpu
from jax.sharding import PartitionSpec as P

MESH = pl.DeviceIdType.MESH
NY = 4
NZ = 8
BLOCKS = 8
NEAR = 5


def slot_of(dz):
    return (dz + 2) % NZ


def kernel(
    panels,
    rhs_hbm,
    fronts_hbm,
    wave_hbm,
    pml_ref,
    field_ref,
    resid_ref,
    rhs_ref,
    wave_ref,
    cs,
    xs,
    piece,
    swept,
    rhs_next,
    before,
    behind,
    above,
    below,
    rhs_sem,
    wave_sem,
    cs_sem,
    a_send,
    d_send,
    a_recv,
    b_send,
    b_recv,
    n_send,
    n_recv,
    h_send,
    h_recv,
):
    blocks = xs.shape[0]
    rows2 = xs.shape[3]
    per = rows2 // 2
    piece_cols = xs.shape[4]
    columns = rhs_ref.shape[1]
    fronts_n = NY * NZ
    groups = (pl.ds(0, NEAR), pl.ds(NEAR, NZ - NEAR))

    q = lax.axis_index("panel")
    f = lax.axis_index("front")
    z = f // NY
    y = f % NY

    def peer(panel, zz, yy):
        return (panel, zz * NY + yy)

    barrier = pltpu.get_barrier_semaphore()

    def greet(device):
        pl.semaphore_signal(barrier, inc=1, device_id=device, device_id_type=MESH)

    targets = (
        ((4, 0), (3, 0), (5, 0), (2, 0), (6, 0), (4, 2), (3, 2), (5, 2), (1, 0), (7, 0), (0, 0))
    )

    def target(panel, j, k):
        return peer(panel, (z + j) % NZ, (y + k) % NY)

    @pl.when(q == 0)
    def _():
        for j, k in targets[:-1]:
            greet(target(q, j, k))

    @pl.when(q < panels - 1)
    def _():
        for j, k in targets:
            greet(target(q + 1, j, k))

    @pl.when(q > 0)
    def _():
        for j, k in targets:
            greet(target(q - 1, j, k))

    for k in range(1, NY):
        greet(peer(q, z, (y + k) % NY))

    @pl.when(f > 0)
    def _():
        greet((q, f - 1))

    @pl.when(f < fronts_n - 1)
    def _():
        greet((q, f + 1))

    rhs_in = pltpu.make_async_copy(rhs_hbm, rhs_ref, rhs_sem)
    wave_in = pltpu.make_async_copy(wave_hbm, wave_ref, wave_sem)
    rhs_in.start()
    wave_in.start()

    @pl.loop(0, fronts_n)
    def _(k):
        dy = k // NZ
        slot = k % NZ
        at = ((z + slot + NZ - 2) % NZ) * NY + (y + dy) % NY
        pltpu.make_async_copy(
            fronts_hbm.at[:, :, pl.ds(pl.multiple_of(at * piece_cols, piece_cols), piece_cols)],
            cs.at[dy, :, :, pl.ds(pl.multiple_of(slot * piece_cols, piece_cols), piece_cols)],
            cs_sem,
        ).start()

    def rhs_rows(ref, b, row, part):
        return ref[pl.ds(b * (per * 4) + row * 2 + part, per, stride=4), :]

    def as_piece(b, ref, field):
        parts = []
        for part in range(2):
            halves = [rhs_rows(ref, b, row, part) for row in range(2)]
            value = jnp.concatenate(halves, axis=1)
            if field is not None:
                value = value + field[part]
            parts.append(value)
        return jnp.concatenate(parts, axis=0).astype(jnp.bfloat16)

    rhs_in.wait()

    @pl.when(q == 0)
    def _():
        @pl.loop(0, blocks)
        def _(b):
            piece[b] = as_piece(b, rhs_ref, None)

    @pl.when(f == 0)
    def _():
        above[...] = jnp.zeros_like(above)

    @pl.when(f == fronts_n - 1)
    def _():
        below[...] = jnp.zeros_like(below)

    @pl.when(q == 0)
    def _():
        before[...] = jnp.zeros_like(before)

    @pl.when(q == panels - 1)
    def _():
        behind[...] = jnp.zeros_like(behind)

    expected = (
        NY
        - 1
        + jnp.where(q > 0, len(targets), len(targets) - 1)
        + jnp.where(q < panels - 1, len(targets), 0)
        + jnp.where(f > 0, 1, 0)
        + jnp.where(f < fronts_n - 1, 1, 0)
    )
    pl.semaphore_wait(barrier, expected)

    def send_piece(b, source, panel, j, k):
        slot = slot_of(-j % NZ)
        return pltpu.make_async_remote_copy(
            src_ref=piece.at[source],
            dst_ref=xs.at[b, -k % NY, slot],
            send_sem=a_send.at[source] if k == 0 else d_send.at[source],
            recv_sem=a_recv.at[b, 0 if slot < NEAR else 1] if k == 0 else b_recv.at[b, -k % NY, 1],
            device_id=target(panel, j, k),
            device_id_type=MESH,
        )

    @pl.when(q == 0)
    def _():
        @pl.loop(0, blocks)
        def _(b):
            for j, k in targets[:-1]:
                send_piece(b, b, q, j, k).start()
            own = xs.at[b, 0, slot_of(0)]
            pltpu.make_async_copy(piece.at[b], own, a_recv.at[b, 0]).start()

    def send_rhs():
        return pltpu.make_async_remote_copy(
            src_ref=rhs_ref,
            dst_ref=rhs_next,
            send_sem=n_send,
            recv_sem=n_recv,
            device_id=(q - 1, f),
            device_id_type=MESH,
        )

    @pl.when(q > 0)
    def _():
        send_rhs().start()

    to_y = ((2, 1, 3), (1, 3))

    def send_group(b, k, g):
        dy = -k % NY
        return pltpu.make_async_remote_copy(
            src_ref=xs.at[b, 0, groups[g]],
            dst_ref=xs.at[b, dy, groups[g]],
            send_sem=b_send.at[b, k, g],
            recv_sem=b_recv.at[b, dy, g],
            device_id=peer(q, z, (y + k) % NY),
            device_id_type=MESH,
        )

    def bytes_wait(ref, sem):
        pltpu.make_async_copy(ref, ref, sem).wait()

    def forward(b, g):
        bytes_wait(xs.at[b, 0, groups[g]], a_recv.at[b, g])
        for k in to_y[g]:
            send_group(b, k, g).start()

    def times_front(b, dy, g):
        lo, hi = (0, NEAR) if g == 0 else (NEAR, NZ)
        vectors = jnp.concatenate([xs[b, dy, slot] for slot in range(lo, hi)], axis=1)
        block = cs[dy, :, :, lo * piece_cols : hi * piece_cols]
        return lax.dot_general(
            vectors,
            block.reshape(2 * piece_cols, (hi - lo) * piece_cols),
            (((1,), (1,)), ((), ())),
            preferred_element_type=jnp.float32,
        )

    def arrived(b, dy, g):
        bytes_wait(xs.at[b, dy, groups[g]], b_recv.at[b, dy, g])
        return times_front(b, dy, g)

    has_before, has_behind = q > 0, q < panels - 1
    has_above, has_below = f > 0, f < fronts_n - 1
    parts_of = (pl.ds(0, blocks - 1), pl.ds(blocks - 1, 1))

    def halos(p):
        def halo(src, dst, at, target):
            return pltpu.make_async_remote_copy(
                src_ref=src,
                dst_ref=dst,
                send_sem=h_send.at[p, at],
                recv_sem=h_recv.at[p, at],
                device_id=target,
                device_id_type=MESH,
            )

        some = parts_of[p]
        return (
            (halo(swept.at[some], behind.at[some], 0, (q - 1, f)), has_before, has_behind),
            (halo(swept.at[some], before.at[some], 1, (q + 1, f)), has_behind, has_before),
            (
                halo(swept.at[some, :, pl.ds(0, columns)], below.at[some], 2, (q, f - 1)),
                has_above,
                has_below,
            ),
            (
                halo(swept.at[some, :, pl.ds(columns, columns)], above.at[some], 3, (q, f + 1)),
                has_below,
                has_above,
            ),
        )

    def send_halos(p):
        for copy, sends, _ in halos(p):
            pl.when(sends)(copy.start)

    forward(0, 0)
    forward(0, 1)
    bytes_wait(cs, cs_sem)

    @pl.when(q < panels - 1)
    def _():
        bytes_wait(rhs_next, n_recv)

    @pl.loop(0, blocks)
    def _(b):
        total = times_front(b, 0, 0) + times_front(b, 0, 1)

        @pl.when(b + 1 < blocks)
        def _():
            forward(b + 1, 0)

        for dy, g in ((1, 0), (3, 0), (2, 1), (2, 0)):
            total = total + arrived(b, dy, g)

        @pl.when(b + 1 < blocks)
        def _():
            forward(b + 1, 1)

        for dy in (1, 3):
            total = total + arrived(b, dy, 1)
        re = total[:per, :piece_cols] - total[per:, piece_cols:]
        im = total[:per, piece_cols:] + total[per:, :piece_cols]

        @pl.when(q < panels - 1)
        def _():
            source = jnp.where(q == 0, blocks + b, b)
            piece[source] = as_piece(b, rhs_next, (re, im))
            for j, k in targets:
                send_piece(b, source, q + 1, j, k).start()

        swept[b] = jnp.concatenate([re, im], axis=0).astype(jnp.bfloat16)
        for part, value in ((0, re), (1, im)):
            for row in range(2):
                field_ref[pl.ds(b * (per * 4) + row * 2 + part, per, stride=4), :] = value[
                    :, row * columns : (row + 1) * columns
                ]

        @pl.when(b == blocks - 2)
        def _():
            send_halos(0)

    send_halos(1)
    wave_in.wait()
    thick = jnp.full((1, columns), pml_ref[0], jnp.int32).astype(jnp.float32)
    last_row = fronts_n * 2 - 1

    def residual_of(p):
        first, count = (0, blocks - 1) if p == 0 else (blocks - 1, 1)
        rhs_count = count * per
        some = parts_of[p]
        for copy, _, receives in halos(p):
            pl.when(receives)(copy.wait_recv)
        lane = lax.broadcasted_iota(jnp.int32, (rhs_count, columns), 1)

        def at(row, part):
            return pl.ds(first * per * 4 + row * 2 + part, rhs_count, stride=4)

        def from_halo(ref, part, lo):
            values = ref[some, :, lo : lo + columns].astype(jnp.float32)
            return values[:, part * per : (part + 1) * per].reshape(rhs_count, columns)

        field = [[field_ref[at(row, part), :] for part in range(2)] for row in range(2)]
        for row in range(2):
            row_pos = jnp.full((1, columns), f * 2 + row, jnp.int32).astype(jnp.float32)
            absorb = (
                2.0
                * (
                    jnp.maximum(0.0, thick - row_pos)
                    + jnp.maximum(0.0, row_pos - (last_row - thick))
                )
                / thick
            )
            diagonal = 6.0 - wave_ref[row : row + 1, :]
            for part in range(2):
                u = field[row][part]
                beside = from_halo(behind, part, row * columns)
                beside = beside + from_halo(before, part, row * columns)
                if row == 0:
                    beside = beside + field[1][part] + from_halo(above, part, 0)
                else:
                    beside = beside + from_halo(below, part, 0) + field[0][part]
                right = jnp.where(lane == columns - 1, 0.0, pltpu.roll(u, columns - 1, 1))
                left = jnp.where(lane == 0, 0.0, pltpu.roll(u, 1, 1))
                beside = beside + right + left
                other = absorb * field[row][1 - part]
                applied = diagonal * u + (other if part == 1 else -other) - beside
                resid_ref[at(row, part), :] = rhs_ref[at(row, part), :] - applied

    residual_of(0)
    residual_of(1)

    for p in range(2):
        for copy, sends, _ in halos(p):
            pl.when(sends)(copy.wait_send)

    @pl.when(q > 0)
    def _():
        send_rhs().wait_send()

    @pl.loop(0, blocks)
    def _(b):
        for g in range(2):
            for k in to_y[g]:
                send_group(b, k, g).wait_send()

        @pl.when(q == 0)
        def _():
            bytes_wait(xs.at[b, 0, pl.ds(0, NZ - 1)], a_send.at[b])
            bytes_wait(xs.at[b, 2, groups[1]], d_send.at[b])

        @pl.when(q < panels - 1)
        def _():
            source = jnp.where(q == 0, blocks + b, b)
            bytes_wait(xs.at[b, 0], a_send.at[source])
            bytes_wait(xs.at[b, 2, groups[1]], d_send.at[source])


def local(rhs, fronts, wave_sq, pml_width):
    _, rhs_count, row_count, components, columns = rhs.shape
    panels = lax.axis_size("panel")
    rows = rhs_count * row_count * components
    piece_cols = row_count * columns
    rows2 = components * rhs_count // BLOCKS
    bf16, f32 = jnp.bfloat16, jnp.float32
    dma = pltpu.SemaphoreType.DMA
    vmem = pl.BlockSpec(memory_space=pltpu.VMEM)
    anywhere = pl.BlockSpec(memory_space=pl.ANY)
    field, resid = pl.pallas_call(
        functools.partial(kernel, panels),
        out_shape=(jax.ShapeDtypeStruct((rows, columns), f32),) * 2,
        in_specs=[anywhere, anywhere, anywhere, pl.BlockSpec(memory_space=pltpu.SMEM)],
        out_specs=(vmem, vmem),
        scratch_shapes=[
            pltpu.VMEM((rows, columns), f32),
            pltpu.VMEM((row_count, columns), f32),
            pltpu.VMEM((NY, 2, piece_cols, NZ * piece_cols), bf16),
            pltpu.VMEM((BLOCKS, NY, NZ, rows2, piece_cols), bf16),
            pltpu.VMEM((2 * BLOCKS, rows2, piece_cols), bf16),
            pltpu.VMEM((BLOCKS, rows2, piece_cols), bf16),
            pltpu.VMEM((rows, columns), f32),
            pltpu.VMEM((BLOCKS, rows2, piece_cols), bf16),
            pltpu.VMEM((BLOCKS, rows2, piece_cols), bf16),
            pltpu.VMEM((BLOCKS, rows2, columns), bf16),
            pltpu.VMEM((BLOCKS, rows2, columns), bf16),
            dma,
            dma,
            dma,
            dma((2 * BLOCKS,)),
            dma((2 * BLOCKS,)),
            dma((BLOCKS, 2)),
            dma((BLOCKS, NY, 2)),
            dma((BLOCKS, NY, 2)),
            dma,
            dma,
            dma((2, 4)),
            dma((2, 4)),
        ],
        compiler_params=pltpu.CompilerParams(
            collective_id=0, has_side_effects=True, vmem_limit_bytes=57 * 1024 * 1024
        ),
    )(
        rhs.reshape(rows, columns),
        fronts.reshape(fronts.shape[1:]),
        wave_sq.reshape(row_count, columns),
        pml_width,
    )
    return field.reshape(rhs.shape), resid.reshape(rhs.shape)


def solution(mesh):
    return jax.shard_map(
        local,
        mesh=mesh,
        in_specs=(
            P("panel", None, "front", None, None),
            P("panel", None, "front", None),
            P("panel", "front", None),
            P("panel"),
        ),
        out_specs=(P("panel", None, "front", None, None), P("panel", None, "front", None, None)),
        check_vma=False,
    )
```

```python
import functools

import jax
import jax.numpy as jnp
from jax import lax
from jax.experimental import pallas as pl
from jax.experimental.pallas import tpu as pltpu
from jax.sharding import PartitionSpec as P

MESH = pl.DeviceIdType.MESH
NY = 4
NZ = 8
BLOCKS = 8
NEAR = 5


def slot_of(dz):
    return (dz + 2) % NZ


def kernel(
    panels,
    rhs_hbm,
    fronts_hbm,
    wave_hbm,
    pml_ref,
    field_ref,
    resid_ref,
    rhs_ref,
    wave_ref,
    cs,
    xs,
    piece,
    swept,
    rhs_next,
    before,
    behind,
    above,
    below,
    rhs_sem,
    wave_sem,
    cs_sem,
    a_send,
    a_recv,
    b_send,
    b_recv,
    n_send,
    n_recv,
    h_send,
    h_recv,
):
    blocks = xs.shape[0]
    rows2 = xs.shape[3]
    per = rows2 // 2
    piece_cols = xs.shape[4]
    columns = rhs_ref.shape[1]
    fronts_n = NY * NZ
    groups = (pl.ds(0, NEAR), pl.ds(NEAR, NZ - NEAR))

    q = lax.axis_index("panel")
    f = lax.axis_index("front")
    z = f // NY
    y = f % NY

    def peer(panel, zz, yy):
        return (panel, zz * NY + yy)

    barrier = pltpu.get_barrier_semaphore()

    def greet(target):
        pl.semaphore_signal(barrier, inc=1, device_id=target, device_id_type=MESH)

    far_first = (4, 3, 5, 2, 6, 1, 7, 0)

    @pl.when(q == 0)
    def _():
        for j in far_first[:-1]:
            greet(peer(q, (z + j) % NZ, y))

    @pl.when(q < panels - 1)
    def _():
        for j in far_first:
            greet(peer(q + 1, (z + j) % NZ, y))

    @pl.when(q > 0)
    def _():
        for j in far_first:
            greet(peer(q - 1, (z + j) % NZ, y))

    for k in range(1, NY):
        greet(peer(q, z, (y + k) % NY))

    @pl.when(f > 0)
    def _():
        greet((q, f - 1))

    @pl.when(f < fronts_n - 1)
    def _():
        greet((q, f + 1))

    rhs_in = pltpu.make_async_copy(rhs_hbm, rhs_ref, rhs_sem)
    wave_in = pltpu.make_async_copy(wave_hbm, wave_ref, wave_sem)
    rhs_in.start()
    wave_in.start()

    @pl.loop(0, fronts_n)
    def _(k):
        dy = k // NZ
        slot = k % NZ
        at = ((z + slot + NZ - 2) % NZ) * NY + (y + dy) % NY
        pltpu.make_async_copy(
            fronts_hbm.at[:, :, pl.ds(pl.multiple_of(at * piece_cols, piece_cols), piece_cols)],
            cs.at[dy, :, :, pl.ds(pl.multiple_of(slot * piece_cols, piece_cols), piece_cols)],
            cs_sem,
        ).start()

    def rhs_rows(ref, b, row, part):
        return ref[pl.ds(b * (per * 4) + row * 2 + part, per, stride=4), :]

    def as_piece(b, ref, field):
        parts = []
        for part in range(2):
            halves = [rhs_rows(ref, b, row, part) for row in range(2)]
            value = jnp.concatenate(halves, axis=1)
            if field is not None:
                value = value + field[part]
            parts.append(value)
        return jnp.concatenate(parts, axis=0).astype(jnp.bfloat16)

    rhs_in.wait()

    @pl.when(q == 0)
    def _():
        @pl.loop(0, blocks)
        def _(b):
            piece[b] = as_piece(b, rhs_ref, None)

    @pl.when(f == 0)
    def _():
        above[...] = jnp.zeros_like(above)

    @pl.when(f == fronts_n - 1)
    def _():
        below[...] = jnp.zeros_like(below)

    @pl.when(q == 0)
    def _():
        before[...] = jnp.zeros_like(before)

    @pl.when(q == panels - 1)
    def _():
        behind[...] = jnp.zeros_like(behind)

    expected = (
        NY
        - 1
        + jnp.where(q > 0, NZ, NZ - 1)
        + jnp.where(q < panels - 1, NZ, 0)
        + jnp.where(f > 0, 1, 0)
        + jnp.where(f < fronts_n - 1, 1, 0)
    )
    pl.semaphore_wait(barrier, expected)

    def send_piece(b, source, panel, j):
        slot = slot_of(-j % NZ)
        return pltpu.make_async_remote_copy(
            src_ref=piece.at[source],
            dst_ref=xs.at[b, 0, slot],
            send_sem=a_send.at[source],
            recv_sem=a_recv.at[b, 0 if slot < NEAR else 1],
            device_id=peer(panel, (z + j) % NZ, y),
            device_id_type=MESH,
        )

    @pl.when(q == 0)
    def _():
        @pl.loop(0, blocks)
        def _(b):
            for j in far_first[:-1]:
                send_piece(b, b, q, j).start()
            own = xs.at[b, 0, slot_of(0)]
            pltpu.make_async_copy(piece.at[b], own, a_recv.at[b, 0]).start()

    def send_rhs():
        return pltpu.make_async_remote_copy(
            src_ref=rhs_ref,
            dst_ref=rhs_next,
            send_sem=n_send,
            recv_sem=n_recv,
            device_id=(q - 1, f),
            device_id_type=MESH,
        )

    @pl.when(q > 0)
    def _():
        send_rhs().start()

    def send_group(b, k, g):
        dy = -k % NY
        return pltpu.make_async_remote_copy(
            src_ref=xs.at[b, 0, groups[g]],
            dst_ref=xs.at[b, dy, groups[g]],
            send_sem=b_send.at[b, k, g],
            recv_sem=b_recv.at[b, dy, g],
            device_id=peer(q, z, (y + k) % NY),
            device_id_type=MESH,
        )

    def bytes_wait(ref, sem):
        pltpu.make_async_copy(ref, ref, sem).wait()

    def forward(b, g):
        bytes_wait(xs.at[b, 0, groups[g]], a_recv.at[b, g])
        for k in (2, 1, 3):
            send_group(b, k, g).start()

    def times_front(b, dy, g):
        lo, hi = (0, NEAR) if g == 0 else (NEAR, NZ)
        vectors = jnp.concatenate([xs[b, dy, slot] for slot in range(lo, hi)], axis=1)
        block = cs[dy, :, :, lo * piece_cols : hi * piece_cols]
        return lax.dot_general(
            vectors,
            block.reshape(2 * piece_cols, (hi - lo) * piece_cols),
            (((1,), (1,)), ((), ())),
            preferred_element_type=jnp.float32,
        )

    def arrived(b, dy, g):
        bytes_wait(xs.at[b, dy, groups[g]], b_recv.at[b, dy, g])
        return times_front(b, dy, g)

    has_before, has_behind = q > 0, q < panels - 1
    has_above, has_below = f > 0, f < fronts_n - 1
    cuts = (0, blocks // 2, blocks * 3 // 4, blocks)
    parts_of = [pl.ds(cuts[p], cuts[p + 1] - cuts[p]) for p in range(3)]

    def halos(p):
        def halo(src, dst, at, target):
            return pltpu.make_async_remote_copy(
                src_ref=src,
                dst_ref=dst,
                send_sem=h_send.at[p, at],
                recv_sem=h_recv.at[p, at],
                device_id=target,
                device_id_type=MESH,
            )

        some = parts_of[p]
        return (
            (halo(swept.at[some], behind.at[some], 0, (q - 1, f)), has_before, has_behind),
            (halo(swept.at[some], before.at[some], 1, (q + 1, f)), has_behind, has_before),
            (
                halo(swept.at[some, :, pl.ds(0, columns)], below.at[some], 2, (q, f - 1)),
                has_above,
                has_below,
            ),
            (
                halo(swept.at[some, :, pl.ds(columns, columns)], above.at[some], 3, (q, f + 1)),
                has_below,
                has_above,
            ),
        )

    def send_halos(p):
        for copy, sends, _ in halos(p):
            pl.when(sends)(copy.start)

    forward(0, 0)
    forward(0, 1)
    bytes_wait(cs, cs_sem)

    @pl.when(q < panels - 1)
    def _():
        bytes_wait(rhs_next, n_recv)

    wave_in.wait()
    thick = jnp.full((1, columns), pml_ref[0], jnp.int32).astype(jnp.float32)
    last_row = fronts_n * 2 - 1

    def residual_of(p):
        first, count = cuts[p], cuts[p + 1] - cuts[p]
        rhs_count = count * per
        some = parts_of[p]
        for copy, _, receives in halos(p):
            pl.when(receives)(copy.wait_recv)
        lane = lax.broadcasted_iota(jnp.int32, (rhs_count, columns), 1)

        def at(row, part):
            return pl.ds(first * per * 4 + row * 2 + part, rhs_count, stride=4)

        def from_halo(ref, part, lo):
            values = ref[some, :, lo : lo + columns].astype(jnp.float32)
            return values[:, part * per : (part + 1) * per].reshape(rhs_count, columns)

        field = [[field_ref[at(row, part), :] for part in range(2)] for row in range(2)]
        for row in range(2):
            row_pos = jnp.full((1, columns), f * 2 + row, jnp.int32).astype(jnp.float32)
            absorb = (
                2.0
                * (
                    jnp.maximum(0.0, thick - row_pos)
                    + jnp.maximum(0.0, row_pos - (last_row - thick))
                )
                / thick
            )
            diagonal = 6.0 - wave_ref[row : row + 1, :]
            for part in range(2):
                u = field[row][part]
                beside = from_halo(behind, part, row * columns)
                beside = beside + from_halo(before, part, row * columns)
                if row == 0:
                    beside = beside + field[1][part] + from_halo(above, part, 0)
                else:
                    beside = beside + from_halo(below, part, 0) + field[0][part]
                right = jnp.where(lane == columns - 1, 0.0, pltpu.roll(u, columns - 1, 1))
                left = jnp.where(lane == 0, 0.0, pltpu.roll(u, 1, 1))
                beside = beside + right + left
                other = absorb * field[row][1 - part]
                applied = diagonal * u + (other if part == 1 else -other) - beside
                resid_ref[at(row, part), :] = rhs_ref[at(row, part), :] - applied

    @pl.loop(0, blocks)
    def _(b):
        total = times_front(b, 0, 0) + times_front(b, 0, 1)

        @pl.when(b + 1 < blocks)
        def _():
            forward(b + 1, 0)

        for p in range(2):
            pl.when((q == panels - 1) & (b == cuts[p + 1] + 1))(functools.partial(residual_of, p))

        for dy in (1, 3, 2):
            total = total + arrived(b, dy, 0)

        @pl.when(b + 1 < blocks)
        def _():
            forward(b + 1, 1)

        for dy in (1, 3, 2):
            total = total + arrived(b, dy, 1)
        re = total[:per, :piece_cols] - total[per:, piece_cols:]
        im = total[:per, piece_cols:] + total[per:, :piece_cols]

        @pl.when(q < panels - 1)
        def _():
            source = jnp.where(q == 0, blocks + b, b)
            piece[source] = as_piece(b, rhs_next, (re, im))
            for j in far_first:
                send_piece(b, source, q + 1, j).start()

        swept[b] = jnp.concatenate([re, im], axis=0).astype(jnp.bfloat16)
        for part, value in ((0, re), (1, im)):
            for row in range(2):
                field_ref[pl.ds(b * (per * 4) + row * 2 + part, per, stride=4), :] = value[
                    :, row * columns : (row + 1) * columns
                ]

        for p in range(2):
            pl.when(b == cuts[p + 1] - 1)(functools.partial(send_halos, p))

    send_halos(2)

    @pl.when(q < panels - 1)
    def _():
        residual_of(0)
        residual_of(1)

    residual_of(2)

    for p in range(3):
        for copy, sends, _ in halos(p):
            pl.when(sends)(copy.wait_send)

    @pl.when(q > 0)
    def _():
        send_rhs().wait_send()

    @pl.loop(0, blocks)
    def _(b):
        for g in range(2):
            for k in range(1, NY):
                send_group(b, k, g).wait_send()

        @pl.when(q == 0)
        def _():
            bytes_wait(xs.at[b, 0, pl.ds(0, NZ - 1)], a_send.at[b])

        @pl.when(q < panels - 1)
        def _():
            bytes_wait(xs.at[b, 0], a_send.at[jnp.where(q == 0, blocks + b, b)])


def local(rhs, fronts, wave_sq, pml_width):
    _, rhs_count, row_count, components, columns = rhs.shape
    panels = lax.axis_size("panel")
    rows = rhs_count * row_count * components
    piece_cols = row_count * columns
    rows2 = components * rhs_count // BLOCKS
    bf16, f32 = jnp.bfloat16, jnp.float32
    dma = pltpu.SemaphoreType.DMA
    vmem = pl.BlockSpec(memory_space=pltpu.VMEM)
    anywhere = pl.BlockSpec(memory_space=pl.ANY)
    field, resid = pl.pallas_call(
        functools.partial(kernel, panels),
        out_shape=(jax.ShapeDtypeStruct((rows, columns), f32),) * 2,
        in_specs=[anywhere, anywhere, anywhere, pl.BlockSpec(memory_space=pltpu.SMEM)],
        out_specs=(vmem, vmem),
        scratch_shapes=[
            pltpu.VMEM((rows, columns), f32),
            pltpu.VMEM((row_count, columns), f32),
            pltpu.VMEM((NY, 2, piece_cols, NZ * piece_cols), bf16),
            pltpu.VMEM((BLOCKS, NY, NZ, rows2, piece_cols), bf16),
            pltpu.VMEM((2 * BLOCKS, rows2, piece_cols), bf16),
            pltpu.VMEM((BLOCKS, rows2, piece_cols), bf16),
            pltpu.VMEM((rows, columns), f32),
            pltpu.VMEM((BLOCKS, rows2, piece_cols), bf16),
            pltpu.VMEM((BLOCKS, rows2, piece_cols), bf16),
            pltpu.VMEM((BLOCKS, rows2, columns), bf16),
            pltpu.VMEM((BLOCKS, rows2, columns), bf16),
            dma,
            dma,
            dma,
            dma((2 * BLOCKS,)),
            dma((BLOCKS, 2)),
            dma((BLOCKS, NY, 2)),
            dma((BLOCKS, NY, 2)),
            dma,
            dma,
            dma((3, 4)),
            dma((3, 4)),
        ],
        compiler_params=pltpu.CompilerParams(
            collective_id=0, has_side_effects=True, vmem_limit_bytes=48 * 1024 * 1024
        ),
    )(
        pltpu.with_memory_space_constraint(rhs.reshape(rows, columns), pltpu.HBM),
        fronts.reshape(fronts.shape[1:]),
        pltpu.with_memory_space_constraint(wave_sq.reshape(row_count, columns), pltpu.HBM),
        pml_width,
    )
    return field.reshape(rhs.shape), resid.reshape(rhs.shape)


def solution(mesh):
    return jax.shard_map(
        local,
        mesh=mesh,
        in_specs=(
            P("panel", None, "front", None, None),
            P("panel", None, "front", None),
            P("panel", "front", None),
            P("panel"),
        ),
        out_specs=(P("panel", None, "front", None, None), P("panel", None, "front", None, None)),
        check_vma=False,
    )
```

```python
import functools

import jax
import jax.numpy as jnp
from jax import lax
from jax.experimental import pallas as pl
from jax.experimental.pallas import tpu as pltpu
from jax.sharding import PartitionSpec as P

MESH = pl.DeviceIdType.MESH
NY = 4
NZ = 8
BLOCKS = 8
NEAR = 5


def slot_of(dz):
    return (dz + 2) % NZ


def kernel(
    panels,
    rhs_hbm,
    fronts_hbm,
    wave_hbm,
    pml_ref,
    field_ref,
    resid_ref,
    rhs_ref,
    wave_ref,
    cs,
    xs,
    piece,
    swept,
    rhs_next,
    before,
    behind,
    above,
    below,
    rhs_sem,
    wave_sem,
    cs_sem,
    a_send,
    a_recv,
    b_send,
    b_recv,
    n_send,
    n_recv,
    h_send,
    h_recv,
):
    blocks = xs.shape[0]
    rows2 = xs.shape[3]
    per = rows2 // 2
    piece_cols = xs.shape[4]
    columns = rhs_ref.shape[1]
    fronts_n = NY * NZ
    groups = (pl.ds(0, NEAR), pl.ds(NEAR, NZ - NEAR))

    q = lax.axis_index("panel")
    f = lax.axis_index("front")
    z = f // NY
    y = f % NY

    def peer(panel, zz, yy):
        return (panel, zz * NY + yy)

    barrier = pltpu.get_barrier_semaphore()

    def greet(target):
        pl.semaphore_signal(barrier, inc=1, device_id=target, device_id_type=MESH)

    far_first = (4, 3, 5, 2, 6, 1, 7, 0)

    @pl.when(q == 0)
    def _():
        for j in far_first[:-1]:
            greet(peer(q, (z + j) % NZ, y))

    @pl.when(q < panels - 1)
    def _():
        for j in far_first:
            greet(peer(q + 1, (z + j) % NZ, y))

    @pl.when(q > 0)
    def _():
        for j in far_first:
            greet(peer(q - 1, (z + j) % NZ, y))

    for k in range(1, NY):
        greet(peer(q, z, (y + k) % NY))

    @pl.when(f > 0)
    def _():
        greet((q, f - 1))

    @pl.when(f < fronts_n - 1)
    def _():
        greet((q, f + 1))

    rhs_in = pltpu.make_async_copy(rhs_hbm, rhs_ref, rhs_sem)
    wave_in = pltpu.make_async_copy(wave_hbm, wave_ref, wave_sem)
    rhs_in.start()
    wave_in.start()

    @pl.loop(0, fronts_n)
    def _(k):
        dy = k // NZ
        slot = k % NZ
        at = ((z + slot + NZ - 2) % NZ) * NY + (y + dy) % NY
        pltpu.make_async_copy(
            fronts_hbm.at[:, :, pl.ds(pl.multiple_of(at * piece_cols, piece_cols), piece_cols)],
            cs.at[dy, :, :, pl.ds(pl.multiple_of(slot * piece_cols, piece_cols), piece_cols)],
            cs_sem,
        ).start()

    def rhs_rows(ref, b, row, part):
        return ref[pl.ds(b * (per * 4) + row * 2 + part, per, stride=4), :]

    def as_piece(b, ref, field):
        parts = []
        for part in range(2):
            halves = [rhs_rows(ref, b, row, part) for row in range(2)]
            value = jnp.concatenate(halves, axis=1)
            if field is not None:
                value = value + field[part]
            parts.append(value)
        return jnp.concatenate(parts, axis=0).astype(jnp.bfloat16)

    rhs_in.wait()

    @pl.when(q == 0)
    def _():
        @pl.loop(0, blocks)
        def _(b):
            piece[b] = as_piece(b, rhs_ref, None)

    @pl.when(f == 0)
    def _():
        above[...] = jnp.zeros_like(above)

    @pl.when(f == fronts_n - 1)
    def _():
        below[...] = jnp.zeros_like(below)

    @pl.when(q == 0)
    def _():
        before[...] = jnp.zeros_like(before)

    @pl.when(q == panels - 1)
    def _():
        behind[...] = jnp.zeros_like(behind)

    expected = (
        NY
        - 1
        + jnp.where(q > 0, NZ, NZ - 1)
        + jnp.where(q < panels - 1, NZ, 0)
        + jnp.where(f > 0, 1, 0)
        + jnp.where(f < fronts_n - 1, 1, 0)
    )
    pl.semaphore_wait(barrier, expected)

    def send_piece(b, source, panel, j):
        slot = slot_of(-j % NZ)
        return pltpu.make_async_remote_copy(
            src_ref=piece.at[source],
            dst_ref=xs.at[b, 0, slot],
            send_sem=a_send.at[source],
            recv_sem=a_recv.at[b, 0 if slot < NEAR else 1],
            device_id=peer(panel, (z + j) % NZ, y),
            device_id_type=MESH,
        )

    @pl.when(q == 0)
    def _():
        @pl.loop(0, blocks)
        def _(b):
            for j in far_first[:-1]:
                send_piece(b, b, q, j).start()
            own = xs.at[b, 0, slot_of(0)]
            pltpu.make_async_copy(piece.at[b], own, a_recv.at[b, 0]).start()

    def send_rhs():
        return pltpu.make_async_remote_copy(
            src_ref=rhs_ref,
            dst_ref=rhs_next,
            send_sem=n_send,
            recv_sem=n_recv,
            device_id=(q - 1, f),
            device_id_type=MESH,
        )

    @pl.when(q > 0)
    def _():
        send_rhs().start()

    def send_group(b, k, g):
        dy = -k % NY
        return pltpu.make_async_remote_copy(
            src_ref=xs.at[b, 0, groups[g]],
            dst_ref=xs.at[b, dy, groups[g]],
            send_sem=b_send.at[b, k, g],
            recv_sem=b_recv.at[b, dy, g],
            device_id=peer(q, z, (y + k) % NY),
            device_id_type=MESH,
        )

    def bytes_wait(ref, sem):
        pltpu.make_async_copy(ref, ref, sem).wait()

    def forward(b, g):
        bytes_wait(xs.at[b, 0, groups[g]], a_recv.at[b, g])
        for k in (2, 1, 3):
            send_group(b, k, g).start()

    def times_front(b, dy, g):
        lo, hi = (0, NEAR) if g == 0 else (NEAR, NZ)
        vectors = jnp.concatenate([xs[b, dy, slot] for slot in range(lo, hi)], axis=1)
        block = cs[dy, :, :, lo * piece_cols : hi * piece_cols]
        return lax.dot_general(
            vectors,
            block.reshape(2 * piece_cols, (hi - lo) * piece_cols),
            (((1,), (1,)), ((), ())),
            preferred_element_type=jnp.float32,
        )

    def arrived(b, dy, g):
        bytes_wait(xs.at[b, dy, groups[g]], b_recv.at[b, dy, g])
        return times_front(b, dy, g)

    has_before, has_behind = q > 0, q < panels - 1
    has_above, has_below = f > 0, f < fronts_n - 1
    cuts = (0, blocks // 2, blocks * 3 // 4, blocks)
    parts_of = [pl.ds(cuts[p], cuts[p + 1] - cuts[p]) for p in range(3)]

    def halos(p):
        def halo(src, dst, at, target):
            return pltpu.make_async_remote_copy(
                src_ref=src,
                dst_ref=dst,
                send_sem=h_send.at[p, at],
                recv_sem=h_recv.at[p, at],
                device_id=target,
                device_id_type=MESH,
            )

        some = parts_of[p]
        return (
            (halo(swept.at[some], behind.at[some], 0, (q - 1, f)), has_before, has_behind),
            (halo(swept.at[some], before.at[some], 1, (q + 1, f)), has_behind, has_before),
            (
                halo(swept.at[some, :, pl.ds(0, columns)], below.at[some], 2, (q, f - 1)),
                has_above,
                has_below,
            ),
            (
                halo(swept.at[some, :, pl.ds(columns, columns)], above.at[some], 3, (q, f + 1)),
                has_below,
                has_above,
            ),
        )

    def send_halos(p):
        for copy, sends, _ in halos(p):
            pl.when(sends)(copy.start)

    forward(0, 0)
    forward(0, 1)
    bytes_wait(cs, cs_sem)

    @pl.when(q < panels - 1)
    def _():
        bytes_wait(rhs_next, n_recv)

    wave_in.wait()
    thick = jnp.full((1, columns), pml_ref[0], jnp.int32).astype(jnp.float32)
    last_row = fronts_n * 2 - 1

    def residual_of(p):
        first, count = cuts[p], cuts[p + 1] - cuts[p]
        rhs_count = count * per
        some = parts_of[p]
        for copy, _, receives in halos(p):
            pl.when(receives)(copy.wait_recv)
        lane = lax.broadcasted_iota(jnp.int32, (rhs_count, columns), 1)

        def at(row, part):
            return pl.ds(first * per * 4 + row * 2 + part, rhs_count, stride=4)

        def from_halo(ref, part, lo):
            values = ref[some, :, lo : lo + columns].astype(jnp.float32)
            return values[:, part * per : (part + 1) * per].reshape(rhs_count, columns)

        field = [[field_ref[at(row, part), :] for part in range(2)] for row in range(2)]
        for row in range(2):
            row_pos = jnp.full((1, columns), f * 2 + row, jnp.int32).astype(jnp.float32)
            absorb = (
                2.0
                * (
                    jnp.maximum(0.0, thick - row_pos)
                    + jnp.maximum(0.0, row_pos - (last_row - thick))
                )
                / thick
            )
            diagonal = 6.0 - wave_ref[row : row + 1, :]
            for part in range(2):
                u = field[row][part]
                beside = from_halo(behind, part, row * columns)
                beside = beside + from_halo(before, part, row * columns)
                if row == 0:
                    beside = beside + field[1][part] + from_halo(above, part, 0)
                else:
                    beside = beside + from_halo(below, part, 0) + field[0][part]
                right = jnp.where(lane == columns - 1, 0.0, pltpu.roll(u, columns - 1, 1))
                left = jnp.where(lane == 0, 0.0, pltpu.roll(u, 1, 1))
                beside = beside + right + left
                other = absorb * field[row][1 - part]
                applied = diagonal * u + (other if part == 1 else -other) - beside
                resid_ref[at(row, part), :] = rhs_ref[at(row, part), :] - applied

    @pl.loop(0, blocks)
    def _(b):
        total = times_front(b, 0, 0) + times_front(b, 0, 1)

        @pl.when(b + 1 < blocks)
        def _():
            forward(b + 1, 0)

        for p in range(2):
            pl.when((q == panels - 1) & (b == cuts[p + 1] + 1))(functools.partial(residual_of, p))

        for dy in (1, 3, 2):
            total = total + arrived(b, dy, 0)

        for dy in (1, 3):
            total = total + arrived(b, dy, 1)

        @pl.when(b + 1 < blocks)
        def _():
            forward(b + 1, 1)

        total = total + arrived(b, 2, 1)
        re = total[:per, :piece_cols] - total[per:, piece_cols:]
        im = total[:per, piece_cols:] + total[per:, :piece_cols]

        @pl.when(q < panels - 1)
        def _():
            source = jnp.where(q == 0, blocks + b, b)
            piece[source] = as_piece(b, rhs_next, (re, im))
            for j in far_first:
                send_piece(b, source, q + 1, j).start()

        swept[b] = jnp.concatenate([re, im], axis=0).astype(jnp.bfloat16)
        for part, value in ((0, re), (1, im)):
            for row in range(2):
                field_ref[pl.ds(b * (per * 4) + row * 2 + part, per, stride=4), :] = value[
                    :, row * columns : (row + 1) * columns
                ]

        for p in range(2):
            pl.when(b == cuts[p + 1] - 1)(functools.partial(send_halos, p))

    send_halos(2)

    @pl.when(q < panels - 1)
    def _():
        residual_of(0)
        residual_of(1)

    residual_of(2)

    for p in range(3):
        for copy, sends, _ in halos(p):
            pl.when(sends)(copy.wait_send)

    @pl.when(q > 0)
    def _():
        send_rhs().wait_send()

    @pl.loop(0, blocks)
    def _(b):
        for g in range(2):
            for k in range(1, NY):
                send_group(b, k, g).wait_send()

        @pl.when(q == 0)
        def _():
            bytes_wait(xs.at[b, 0, pl.ds(0, NZ - 1)], a_send.at[b])

        @pl.when(q < panels - 1)
        def _():
            bytes_wait(xs.at[b, 0], a_send.at[jnp.where(q == 0, blocks + b, b)])


def local(rhs, fronts, wave_sq, pml_width):
    _, rhs_count, row_count, components, columns = rhs.shape
    panels = lax.axis_size("panel")
    rows = rhs_count * row_count * components
    piece_cols = row_count * columns
    rows2 = components * rhs_count // BLOCKS
    bf16, f32 = jnp.bfloat16, jnp.float32
    dma = pltpu.SemaphoreType.DMA
    vmem = pl.BlockSpec(memory_space=pltpu.VMEM)
    anywhere = pl.BlockSpec(memory_space=pl.ANY)
    field, resid = pl.pallas_call(
        functools.partial(kernel, panels),
        out_shape=(jax.ShapeDtypeStruct((rows, columns), f32),) * 2,
        in_specs=[anywhere, anywhere, anywhere, pl.BlockSpec(memory_space=pltpu.SMEM)],
        out_specs=(vmem, vmem),
        scratch_shapes=[
            pltpu.VMEM((rows, columns), f32),
            pltpu.VMEM((row_count, columns), f32),
            pltpu.VMEM((NY, 2, piece_cols, NZ * piece_cols), bf16),
            pltpu.VMEM((BLOCKS, NY, NZ, rows2, piece_cols), bf16),
            pltpu.VMEM((2 * BLOCKS, rows2, piece_cols), bf16),
            pltpu.VMEM((BLOCKS, rows2, piece_cols), bf16),
            pltpu.VMEM((rows, columns), f32),
            pltpu.VMEM((BLOCKS, rows2, piece_cols), bf16),
            pltpu.VMEM((BLOCKS, rows2, piece_cols), bf16),
            pltpu.VMEM((BLOCKS, rows2, columns), bf16),
            pltpu.VMEM((BLOCKS, rows2, columns), bf16),
            dma,
            dma,
            dma,
            dma((2 * BLOCKS,)),
            dma((BLOCKS, 2)),
            dma((BLOCKS, NY, 2)),
            dma((BLOCKS, NY, 2)),
            dma,
            dma,
            dma((3, 4)),
            dma((3, 4)),
        ],
        compiler_params=pltpu.CompilerParams(
            collective_id=0, has_side_effects=True, vmem_limit_bytes=48 * 1024 * 1024
        ),
    )(
        pltpu.with_memory_space_constraint(rhs.reshape(rows, columns), pltpu.HBM),
        fronts.reshape(fronts.shape[1:]),
        pltpu.with_memory_space_constraint(wave_sq.reshape(row_count, columns), pltpu.HBM),
        pml_width,
    )
    return field.reshape(rhs.shape), resid.reshape(rhs.shape)


def solution(mesh):
    return jax.shard_map(
        local,
        mesh=mesh,
        in_specs=(
            P("panel", None, "front", None, None),
            P("panel", None, "front", None),
            P("panel", "front", None),
            P("panel"),
        ),
        out_specs=(P("panel", None, "front", None, None), P("panel", None, "front", None, None)),
        check_vma=False,
    )
```
